32 devices in a mesh: blk: 8 (over z, y), layer: 4 (over x, core).
Axes of the slice: x: 2, y: 2, z: 4, core: 2. Of those that a mesh axis runs over, the one named last changes fastest.
Arguments:
- source: float32 [64, 512, 128], P('layer', 'blk'), may hold values from -18 to 18
- sigma_ref: float32 [64, 512, 128], P('layer', 'blk'), may hold values from 0.3 to 3
- owner: int32 [64, 512], P('layer', 'blk'), may hold values from 0 to 31, as said below
- slot: int32 [64, 512], P('layer', 'blk'), may hold values from 0 to 1023, as said below
- temp_old: float32 [32768, 128], P(('blk', 'layer')), may hold values from 0 to 2
- heat_cap: float32 [32768, 128], P(('blk', 'layer')), may hold values from 0.5 to 4
- conduct: float32 [32768, 128], P(('blk', 'layer')), may hold values from 0.2 to 2
Outputs:
- potential: float32 [64, 512, 128], P('layer', 'blk')
- temp_new: float32 [32768, 128], P(('blk', 'layer'))
The draws below stay inside these ranges and needn't reach their ends.
Inputs may be any that keep to these rules, and one draw needn't show every extreme that they name: Among the 1024 blocks of one electric subdomain, at most 64 name the same owner, and 64 is reached in every subdomain. The pairs (owner, slot) are all different: every owner receives exactly 1024 blocks, one for each of its rows.
All inputs are finite; a program needn't handle non-finite values.
Results may differ from the reference program's by a relative error of at most 0.00002.
Values sent between devices are 32-bit elements; how exact they have to be, the bound alone decides.
A program may use at most 64 MiB of HBM per device.

```python
import math
import jax
import jax.numpy as jnp

CA = 16
CR = 64
RAD = 128
SWEEPS = 3
JACOBI = 2
SECTORS = 8
SLABS = 4
DOMAINS = 32
NBLK = 1024
BLOCKS_EACH = 32
NA = 64
NRG = 512
THERMAL_ROWS = 32768


def intersection_maps(key):
    base_key = jax.random.fold_in(key, 7)
    key_pattern, key_receive, key_send = jax.random.split(base_key, 3)
    quarter = DOMAINS // 4
    pattern = jnp.concatenate([jnp.full((quarter,), 2 * BLOCKS_EACH, jnp.int32), jnp.full((DOMAINS - 2 * quarter,), BLOCKS_EACH, jnp.int32), jnp.zeros((quarter,), jnp.int32)])
    shuffle = jax.random.permutation(key_pattern, DOMAINS).astype(jnp.int32)
    source_ids = jnp.arange(DOMAINS, dtype=jnp.int32)
    counts = pattern[(shuffle[None, :] + source_ids[:, None]) % DOMAINS]
    ends = jnp.cumsum(counts, axis=1)
    places = jnp.arange(NBLK, dtype=jnp.int32)
    target = jax.vmap(lambda row_ends: jnp.searchsorted(row_ends, places, side='right'))(ends).astype(jnp.int32)
    begins = jnp.take_along_axis(ends - counts, target, axis=1)
    within = places[None, :] - begins
    offsets = jnp.cumsum(counts, axis=0) - counts
    base_slot = offsets[source_ids[:, None], target] + within
    receive_perm = jax.vmap(lambda sub_key: jax.random.permutation(sub_key, NBLK))(jax.random.split(key_receive, DOMAINS)).astype(jnp.int32)
    slot_table = receive_perm[target, base_slot]
    send_perm = jax.vmap(lambda sub_key: jax.random.permutation(sub_key, NBLK))(jax.random.split(key_send, DOMAINS)).astype(jnp.int32)
    owner_rows = jnp.take_along_axis(target, send_perm, axis=1)
    slot_rows = jnp.take_along_axis(slot_table, send_perm, axis=1)

    def arrange(values):
        return values.reshape(SECTORS, SLABS, CA, CR).transpose(1, 2, 0, 3).reshape(NA, NRG).astype(jnp.int32)
    return (arrange(owner_rows), arrange(slot_rows))


def draw_owner(key, part):
    return intersection_maps(key)[0]


def draw_slot(key, part):
    return intersection_maps(key)[1]


def draw_source(key, part):
    cycle_pos = jnp.arange(NRG, dtype=jnp.float32) / NRG
    amplitude = 1.0 + 2.0 * cycle_pos
    values = jnp.clip(jax.random.normal(key, (NA, NRG, RAD), jnp.float32), -6.0, 6.0)
    return (values * amplitude[None, :, None]).astype(jnp.float32)


def shard_levels(own_key, dims, pieces, low, high):
    def one(position, shards_of):
        steps = jax.random.uniform(jax.random.fold_in(jax.random.fold_in(own_key, 6), position), (shards_of,), jnp.float32, low / len(pieces), high / len(pieces))
        return jnp.repeat(jnp.exp(steps), dims[position] // shards_of).reshape((-1,) + (1,) * (len(dims) - position - 1))

    level = one(*pieces[0])
    for cut in pieces[1:]:
        level = level * one(*cut)
    return level


def setup_inputs(seed: int = 0) -> dict:
    key_of = jax.random.split(jax.random.key(seed), 8)
    return {
        "source": draw_source(jax.random.fold_in(key_of[7], 71), 0),
        "sigma_ref": jnp.clip(jnp.exp(math.log(3.0) - 2.3025851 * jax.random.uniform(key_of[1], (NA, NRG, RAD), jnp.float32) ** shard_levels(key_of[1], (NA, NRG, RAD), ((0, 4), (1, 8)), -0.2, 0.2)), 0.3, 3.0),
        "owner": draw_owner(jax.random.fold_in(key_of[7], 71), 0),
        "slot": draw_slot(jax.random.fold_in(key_of[7], 71), 0),
        "temp_old": jnp.clip(2.0 * jax.random.uniform(key_of[4], (THERMAL_ROWS, RAD), jnp.float32) ** shard_levels(key_of[4], (THERMAL_ROWS, RAD), ((0, 32),), -0.2, 0.2), 0.0, 2.0),
        "heat_cap": jnp.clip(jnp.exp(math.log(4.0) - 2.0794415 * jax.random.uniform(key_of[5], (THERMAL_ROWS, RAD), jnp.float32) ** shard_levels(key_of[5], (THERMAL_ROWS, RAD), ((0, 32),), -0.2, 0.2)), 0.5, 4.0),
        "conduct": jnp.clip(jnp.exp(math.log(2.0) - 2.3025851 * jax.random.uniform(key_of[6], (THERMAL_ROWS, RAD), jnp.float32) ** shard_levels(key_of[6], (THERMAL_ROWS, RAD), ((0, 32),), -0.2, 0.2)), 0.2, 2.0),
    }


COUPLE = 0.4
THETA = 1.125
DELTA = 0.875


def neighbours(field):
    axial = jnp.pad(field, ((1, 1), (0, 0), (0, 0)))
    radial = jnp.pad(field, ((0, 0), (0, 0), (1, 1)))
    return [axial[2:], axial[:-2], jnp.roll(field, -1, 1), jnp.roll(field, 1, 1), radial[:, :, 2:], radial[:, :, :-2]]


def electric(source, cond_here):
    couplings = [0.5 * (cond_here + other) for other in neighbours(cond_here)]
    diag_sum = couplings[0]
    for coupling in couplings[1:]:
        diag_sum = diag_sum + coupling
    inv_diag = 1.0 / diag_sum

    def operate(field):
        result = jnp.zeros_like(field)
        for coupling, other in zip(couplings, neighbours(field)):
            result = result + coupling * (field - other)
        return result

    ratio = THETA / DELTA
    potential = jnp.zeros_like(source)
    residual = source
    search_dir = inv_diag * residual / THETA
    rho_now = 1.0 / ratio
    for sweep in range(SWEEPS):
        potential = potential + search_dir
        if sweep + 1 < SWEEPS:
            residual = residual - operate(search_dir)
            rho_next = 1.0 / (2.0 * ratio - rho_now)
            search_dir = (rho_next * rho_now) * search_dir + (2.0 * rho_next / DELTA) * (inv_diag * residual)
            rho_now = rho_next
    return potential


def joule(potential, cond_here):
    result = jnp.zeros_like(potential)
    for other in neighbours(potential):
        gap = potential - other
        result = result + 0.5 * gap * gap
    return cond_here * result


def thermal_step(temp_old, heat_cap, conduct, heat):
    faces = 0.5 * (conduct[:, 1:] + conduct[:, :-1])
    edge = jnp.zeros((conduct.shape[0], 1), jnp.float32)
    left_cond = jnp.concatenate([edge, faces], axis=1)
    right_cond = jnp.concatenate([faces, edge], axis=1)
    diag_sum = heat_cap + left_cond + right_cond
    target = heat_cap * temp_old + heat
    current = temp_old
    for sweep in range(JACOBI):
        before = jnp.concatenate([edge, current[:, :-1]], axis=1)
        after = jnp.concatenate([current[:, 1:], edge], axis=1)
        current = (target + left_cond * before + right_cond * after) / diag_sum
    return current


def reference(source, sigma_ref, owner, slot, temp_old, heat_cap, conduct):
    rows_index = (owner * NBLK + slot).reshape(-1).astype(jnp.int32)
    temp_here = jnp.take(temp_old, rows_index, axis=0).reshape(NA, NRG, RAD)
    cond_here = sigma_ref / (1.0 + COUPLE * temp_here)
    potential = electric(source, cond_here)
    power = joule(potential, cond_here)
    total = jnp.sum(power)
    scaled = power * ((NA * NRG * RAD) / total)
    heat = jnp.zeros((THERMAL_ROWS, RAD), jnp.float32).at[rows_index].set(scaled.reshape(-1, RAD))
    temp_new = thermal_step(temp_old, heat_cap, conduct, heat)
    return (potential, temp_new)
```

```python
import jax
import jax.numpy as jnp
from jax import lax
from jax.sharding import PartitionSpec as P

SWEEPS = 3
JACOBI = 2


COUPLE = 0.4
THETA = 1.125
DELTA = 0.875


def with_halo(cells, sides, width, closed):
    for axis, dim in sides:
        count = lax.axis_size(axis)
        ends = count if closed else count - 1
        head = lax.slice_in_dim(cells, 0, width, axis=dim)
        tail = lax.slice_in_dim(cells, cells.shape[dim] - width, cells.shape[dim], axis=dim)
        cells = jnp.concatenate(
            [
                lax.ppermute(tail, axis, [(i, (i + 1) % count) for i in range(ends)]),
                cells,
                lax.ppermute(head, axis, [((i + 1) % count, i) for i in range(ends)]),
            ],
            axis=dim,
        )
    return cells


def neighbours(field):
    slab_pad = with_halo(field, (("layer", 0),), 1, False)
    cycle_pad = with_halo(field, (("blk", 1),), 1, True)
    radial = jnp.pad(field, ((0, 0), (0, 0), (1, 1)))
    return [
        slab_pad[2:],
        slab_pad[:-2],
        cycle_pad[:, 2:],
        cycle_pad[:, :-2],
        radial[:, :, 2:],
        radial[:, :, :-2],
    ]


def electric(source, cond_here):
    couplings = [0.5 * (cond_here + other) for other in neighbours(cond_here)]
    diag_sum = couplings[0]
    for coupling in couplings[1:]:
        diag_sum = diag_sum + coupling
    inv_diag = 1.0 / diag_sum
    ratio = THETA / DELTA
    potential = jnp.zeros_like(source)
    residual = source
    search_dir = inv_diag * residual / THETA
    rho_now = 1.0 / ratio
    for sweep in range(SWEEPS):
        potential = potential + search_dir
        if sweep + 1 < SWEEPS:
            result = jnp.zeros_like(search_dir)
            for operate_coupling, operate_other in zip(couplings, neighbours(search_dir)):
                result = result + operate_coupling * (search_dir - operate_other)
            residual = residual - result
            rho_next = 1.0 / (2.0 * ratio - rho_now)
            search_dir = rho_next * rho_now * search_dir + 2.0 * rho_next / DELTA * (
                inv_diag * residual
            )
            rho_now = rho_next
    return potential


def joule(potential, cond_here):
    result = jnp.zeros_like(potential)
    for other in neighbours(potential):
        gap = potential - other
        result = result + 0.5 * gap * gap
    return cond_here * result


def thermal_step(temp_old, heat_cap, conduct, heat):
    faces = 0.5 * (conduct[:, 1:] + conduct[:, :-1])
    edge = jnp.zeros((conduct.shape[0], 1), jnp.float32)
    left_cond = jnp.concatenate([edge, faces], axis=1)
    right_cond = jnp.concatenate([faces, edge], axis=1)
    diag_sum = heat_cap + left_cond + right_cond
    target = heat_cap * temp_old + heat
    current = temp_old
    for sweep in range(JACOBI):
        before = jnp.concatenate([edge, current[:, :-1]], axis=1)
        after = jnp.concatenate([current[:, 1:], edge], axis=1)
        current = (target + left_cond * before + right_cond * after) / diag_sum
    return current


def routing(owner, slot, peers):
    owners = owner.reshape(-1)
    slots = slot.reshape(-1)
    count = owners.shape[0]
    capacity = 2 * count // peers
    named = owners[:, None] == jnp.arange(peers, dtype=jnp.int32)[None, :]
    named_bf = named.astype(jnp.bfloat16)
    order = jnp.arange(count, dtype=jnp.int32)
    earlier = (order[None, :] < order[:, None]).astype(jnp.bfloat16)
    before = jnp.dot(earlier, named_bf, preferred_element_type=jnp.float32)
    within = jnp.sum(jnp.where(named, before, 0.0), axis=1).astype(jnp.int32)
    here = within[:, None] == jnp.arange(capacity, dtype=jnp.int32)[None, :]
    parts = []
    for code in (slots + 1, order + 1):
        for digit in (code >> 5, code & 31):
            parts.append(jnp.where(here, digit[:, None].astype(jnp.float32), 0.0))
    table = jnp.concatenate(parts, axis=1).astype(jnp.bfloat16)
    digits = lax.dot_general(
        named_bf, table, (((0,), (0,)), ((), ())), preferred_element_type=jnp.float32
    ).astype(jnp.int32).reshape(peers, 4, capacity)
    slot_code = digits[:, 0] * 32 + digits[:, 1]
    block_code = digits[:, 2] * 32 + digits[:, 3]
    return owners * capacity + within, slot_code, block_code


def arrivals(slot_code, count):
    code = slot_code.reshape(-1) - 1
    total = code.shape[0]
    place = jnp.arange(total, dtype=jnp.int32)
    low = (code & 31)[:, None] == jnp.arange(32, dtype=jnp.int32)[None, :]
    high = ((code >> 5)[:, None] == jnp.arange(count // 32, dtype=jnp.int32)[None, :])
    table = jnp.concatenate(
        [jnp.where(low, d[:, None].astype(jnp.float32), 0.0) for d in (place >> 5, place & 31)],
        axis=1,
    ).astype(jnp.bfloat16)
    digits = lax.dot_general(
        high.astype(jnp.bfloat16), table, (((0,), (0,)), ((), ())),
        preferred_element_type=jnp.float32,
    ).astype(jnp.int32)
    return (digits[:, :32] * 32 + digits[:, 32:]).reshape(-1)


def swap(rows):
    return lax.all_to_all(rows, ("blk", "layer"), split_axis=0, concat_axis=0, tiled=True)


def per_device(source, sigma_ref, owner, slot, temp_old, heat_cap, conduct):
    peers = lax.axis_size(("blk", "layer"))
    radial = source.shape[2]
    block_count = temp_old.shape[0]
    positions, slot_code, block_code = routing(owner, slot, peers)
    capacity = slot_code.shape[1]
    wanted = swap(slot_code)
    replies = jnp.take(temp_old, jnp.maximum(wanted.reshape(-1) - 1, 0), axis=0, mode="clip")
    fetched = swap(replies.reshape(peers, capacity, radial)).reshape(-1, radial)
    origin = arrivals(wanted, block_count)
    temp_here = jnp.take(fetched, positions, axis=0, mode="clip").reshape(source.shape)
    cond_here = sigma_ref / (1.0 + COUPLE * temp_here)
    potential = electric(source, cond_here)
    power = joule(potential, cond_here)
    total = lax.psum(jnp.sum(power), ("blk", "layer"))
    outgoing = jnp.take(
        power.reshape(-1, radial), jnp.maximum(block_code.reshape(-1) - 1, 0), axis=0, mode="clip"
    )
    arrived = swap(outgoing.reshape(peers, capacity, radial)).reshape(-1, radial)
    factor = source.size * peers / total
    heat = jnp.take(arrived, origin, axis=0, mode="clip") * factor
    temp_new = thermal_step(temp_old, heat_cap, conduct, heat)
    return (potential, temp_new)


def solution(mesh):
    return jax.shard_map(
        per_device,
        mesh=mesh,
        in_specs=(
            P("layer", "blk", None),
            P("layer", "blk", None),
            P("layer", "blk"),
            P("layer", "blk"),
            P(("blk", "layer"), None),
            P(("blk", "layer"), None),
            P(("blk", "layer"), None),
        ),
        out_specs=(P("layer", "blk", None), P(("blk", "layer"), None)),
        check_vma=False,
    )
```

```python
import jax
import jax.numpy as jnp
from jax import lax
from jax.experimental import pallas as pl
from jax.experimental.pallas import tpu as pltpu
from jax.sharding import PartitionSpec as P

SWEEPS = 3
JACOBI = 2


COUPLE = 0.4
THETA = 1.125
DELTA = 0.875


def routing(owner, slot, peers):
    owners = owner.reshape(-1)
    slots = slot.reshape(-1)
    count = owners.shape[0]
    capacity = 2 * count // peers
    named = owners[:, None] == jnp.arange(peers, dtype=jnp.int32)[None, :]
    named_bf = named.astype(jnp.bfloat16)
    order = jnp.arange(count, dtype=jnp.int32)
    earlier = (order[None, :] < order[:, None]).astype(jnp.bfloat16)
    before = jnp.dot(earlier, named_bf, preferred_element_type=jnp.float32)
    within = jnp.sum(jnp.where(named, before, 0.0), axis=1).astype(jnp.int32)
    here = within[:, None] == jnp.arange(capacity, dtype=jnp.int32)[None, :]
    parts = []
    for code in (slots + 1, order + 1):
        for digit in (code >> 5, code & 31):
            parts.append(jnp.where(here, digit[:, None].astype(jnp.float32), 0.0))
    table = jnp.concatenate(parts, axis=1).astype(jnp.bfloat16)
    digits = lax.dot_general(
        named_bf, table, (((0,), (0,)), ((), ())), preferred_element_type=jnp.float32
    ).astype(jnp.int32).reshape(peers, 4, capacity)
    slot_code = digits[:, 0] * 32 + digits[:, 1]
    block_code = digits[:, 2] * 32 + digits[:, 3]
    return owners * capacity + within, slot_code, block_code


WIDE = 4
ROWS = 8
MESH = pl.DeviceIdType.MESH


def shifted(x, step, axis, bounded):
    size = x.shape[axis]
    moved = pltpu.roll(x, step % size, axis)
    if bounded:
        place = lax.broadcasted_iota(jnp.int32, x.shape, axis)
        moved = jnp.where(place == (0 if step > 0 else size - 1), 0.0, moved)
    return moved


def around(ref, e):
    here = ref[e]
    return here, [
        ref[e + 1],
        ref[e - 1],
        shifted(here, -1, 0, False),
        shifted(here, 1, 0, False),
        shifted(here, -1, 1, True),
        shifted(here, 1, 1, True),
    ]


def exchange_kernel(
    layers, blks, slabs,
    source, sigma, temp_old, ask, places, blocks,
    potential, arrived, wanted, sums,
    asked, rows, fetched, src, cond, inv, dir_a, dir_b, res, pot, power, part,
    local_sem, ask_send, ask_recv, row_send, row_recv, pow_send, pow_recv, sum_send, sum_recv,
    halo_send, halo_recv,
):
    n = layers * blks
    cap = blocks.shape[1]
    ca, cr, lanes = source.shape
    blk, layer = lax.axis_index("blk"), lax.axis_index("layer")
    me = blk * layers + layer

    def peer(j):
        return (j // layers, j % layers)

    barrier = pltpu.get_barrier_semaphore()

    def greet(k, carry):
        pl.semaphore_signal(
            barrier, inc=1, device_id=peer(lax.rem(me + k, n)), device_id_type=MESH
        )
        return carry

    lax.fori_loop(1, n, greet, 0)
    own_src = pltpu.make_async_copy(
        source, src.at[pl.ds(WIDE, ca), pl.ds(ROWS, cr)], local_sem.at[0]
    )
    own_src.start()
    own_ask = pltpu.make_async_copy(ask.at[me], wanted.at[me], local_sem.at[1])
    own_ask.start()
    pl.semaphore_wait(barrier, n - 1)

    def remote(src_ref, dst_ref, send, recv, j):
        return pltpu.make_async_remote_copy(
            src_ref=src_ref, dst_ref=dst_ref, send_sem=send, recv_sem=recv,
            device_id=peer(j), device_id_type=MESH,
        )

    def ask_copy(j, slot):
        return remote(ask.at[j], wanted.at[slot], ask_send.at[j], ask_recv.at[slot], j)

    def send_ask(k, carry):
        ask_copy(lax.rem(me + k, n), me).start()
        return carry

    lax.fori_loop(1, n, send_ask, 0)

    directions = [(a, r) for a in (-1, 0, 1) for r in (-1, 0, 1) if (a, r) != (0, 0)]

    def halo(kind, d, field, whole):
        step_a, step_r = directions[d]
        count_a = ca if step_a == 0 else WIDE
        count_r = cr if step_r == 0 else ROWS
        from_a = ca - WIDE if step_a > 0 else 0
        from_r = cr - ROWS if step_r > 0 else 0
        to_a = {0: WIDE, 1: 0, -1: WIDE + ca}[step_a]
        to_r = {0: ROWS, 1: 0, -1: ROWS + cr}[step_r]
        off_a, off_r = (0, 0) if whole is not None else (WIDE, ROWS)
        origin = field if whole is None else whole
        return pltpu.make_async_remote_copy(
            src_ref=origin.at[pl.ds(off_a + from_a, count_a), pl.ds(off_r + from_r, count_r)],
            dst_ref=field.at[pl.ds(to_a, count_a), pl.ds(to_r, count_r)],
            send_sem=halo_send.at[kind, d],
            recv_sem=halo_recv.at[kind, d],
            device_id=(lax.rem(blk + step_r + blks, blks), lax.rem(layer + step_a + layers, layers)),
            device_id_type=MESH,
        )

    def halo_all(kind, field, whole, begin):
        for d, (step_a, _) in enumerate(directions):
            def act(d=d, incoming=False):
                copy = halo(kind, d, field, whole)
                if begin:
                    copy.start()
                elif incoming:
                    copy.wait_recv()
                else:
                    copy.wait_send()

            goes = {0: None, 1: layer < layers - 1, -1: layer > 0}[step_a]
            comes = {0: None, 1: layer > 0, -1: layer < layers - 1}[step_a]
            for cond_here, incoming in ((goes, False), (comes, True)):
                if begin and incoming:
                    continue
                if cond_here is None:
                    act(d, incoming)
                else:
                    pl.when(cond_here)(lambda d=d, incoming=incoming: act(d, incoming))

    halo_all(0, src, source, True)
    own_ask.wait()

    def row_copy(j, slot):
        return remote(
            rows.at[pl.ds(pl.multiple_of(j * cap, 8), cap)],
            fetched.at[pl.ds(pl.multiple_of(slot * cap, 8), cap)],
            row_send.at[j], row_recv.at[slot], j,
        )

    def fill(target, base, table, get):
        for c in range(cap):
            target[pl.ds(base + c, 1), :] = get(jnp.maximum(table(c) - 1, 0))

    def reply(k, carry):
        j = lax.rem(me - k + n, n)

        @pl.when(k > 0)
        def _():
            ask_copy(j, j).wait_recv()

        to_scalar = pltpu.make_async_copy(wanted.at[j], asked.at[j], local_sem.at[2])
        to_scalar.start()
        to_scalar.wait()
        base = pl.multiple_of(j * cap, 8)

        @pl.when(k > 0)
        def _():
            fill(rows, base, lambda c: asked[j, 0, c], lambda i: temp_old[pl.ds(i, 1), :])
            row_copy(j, me).start()

        @pl.when(k == 0)
        def _():
            fill(fetched, base, lambda c: asked[j, 0, c], lambda i: temp_old[pl.ds(i, 1), :])

        return carry

    lax.fori_loop(0, n, reply, 0)

    def got_row(k, carry):
        j = lax.rem(me + k, n)
        row_copy(j, j).wait_recv()
        return carry

    lax.fori_loop(1, n, got_row, 0)

    def place(a, carry):
        for r in range(cr):
            cond[WIDE + a, pl.ds(ROWS + r, 1), :] = fetched[pl.ds(places[a, r], 1), :]
        here = cond[WIDE + a, pl.ds(ROWS, cr), :]
        cond[WIDE + a, pl.ds(ROWS, cr), :] = sigma[a] / (1.0 + COUPLE * here)
        return carry

    lax.fori_loop(0, ca, place, 0)
    halo_all(1, cond, None, True)

    @pl.when(layer == 0)
    def _():
        cond[0:WIDE] = jnp.zeros((WIDE, cr + 2 * ROWS, lanes), jnp.float32)

    @pl.when(layer == layers - 1)
    def _():
        cond[WIDE + ca :] = jnp.zeros((WIDE, cr + 2 * ROWS, lanes), jnp.float32)

    own_src.wait()
    halo_all(0, src, source, False)
    halo_all(1, cond, None, False)

    def inside(e, values):
        at = layer * ca + e - WIDE
        return jnp.where(jnp.logical_and(at >= 0, at < layers * ca), values, 0.0)

    ratio = THETA / DELTA
    rho = [1.0 / ratio]
    for _ in range(2):
        rho.append(1.0 / (2.0 * ratio - rho[-1]))

    def first(e, carry):
        here, others = around(cond, e)
        diag = 0.5 * (here + others[0])
        for other in others[1:]:
            diag = diag + 0.5 * (here + other)
        inverse = 1.0 / diag
        inv[e] = inverse
        dir_a[e] = inside(e, inverse * src[e] / THETA)
        return carry

    lax.fori_loop(1, 2 * WIDE + ca - 1, first, 0)

    def operate(field, e):
        here, others = around(cond, e)
        v, vs = around(field, e)
        result = 0.5 * (here + others[0]) * (v - vs[0])
        for other, other_v in zip(others[1:], vs[1:]):
            result = result + 0.5 * (here + other) * (v - other_v)
        return v, result

    def second(e, carry):
        v, applied = operate(dir_a, e)
        left = src[e] - applied
        res[e] = left
        step = inside(e, (rho[1] * rho[0]) * v + (2.0 * rho[1] / DELTA) * (inv[e] * left))
        dir_b[e] = step
        pot[e] = v + step
        return carry

    lax.fori_loop(2, 2 * WIDE + ca - 2, second, 0)

    def third(e, carry):
        v, applied = operate(dir_b, e)
        left = res[e] - applied
        step = inside(e, (rho[2] * rho[1]) * v + (2.0 * rho[2] / DELTA) * (inv[e] * left))
        pot[e] = pot[e] + step
        return carry

    lax.fori_loop(3, 2 * WIDE + ca - 3, third, 0)

    def joule(a, total):
        v, others = around(pot, a + WIDE)
        result = jnp.zeros_like(v)
        for other in others:
            gap = v - other
            result = result + 0.5 * gap * gap
        result = cond[a + WIDE] * result
        power[pl.ds(pl.multiple_of(a * cr, 8), cr), :] = result[ROWS : ROWS + cr]
        potential[a] = v[ROWS : ROWS + cr]
        return total + jnp.sum(result[ROWS : ROWS + cr], axis=0, keepdims=True)

    part[...] = lax.fori_loop(0, ca, joule, jnp.zeros((1, lanes), jnp.float32))
    sums[me] = part[...]

    def pow_copy(j, slot):
        return remote(
            rows.at[pl.ds(pl.multiple_of(j * cap, 8), cap)],
            arrived.at[pl.ds(pl.multiple_of(slot * cap, 8), cap)],
            pow_send.at[j], pow_recv.at[slot], j,
        )

    def sum_copy(j, slot):
        return remote(part, sums.at[slot], sum_send.at[j], sum_recv.at[slot], j)

    def send_power(k, carry):
        j = lax.rem(me + k, n)
        base = pl.multiple_of(j * cap, 8)

        @pl.when(k < n)
        def _():
            row_copy(j, me).wait_send()
            fill(rows, base, lambda c: blocks[j, c], lambda i: power[pl.ds(i, 1), :])
            pow_copy(j, me).start()
            sum_copy(j, me).start()

        @pl.when(k == n)
        def _():
            fill(arrived, base, lambda c: blocks[j, c], lambda i: power[pl.ds(i, 1), :])

        return carry

    lax.fori_loop(1, n + 1, send_power, 0)

    def finish(k, carry):
        j = lax.rem(me + k, n)
        ask_copy(j, j).wait_send()
        pow_copy(j, j).wait()
        sum_copy(j, j).wait()
        return carry

    lax.fori_loop(1, n, finish, 0)


def thermal_kernel(scale, wanted, arrived, sums, temp_old, heat_cap, conduct, temp_new, heat):
    n, cap = wanted.shape
    count = temp_old.shape[0]
    factor = scale / jnp.sum(sums[...])

    def land(j, carry):
        for c in range(cap):
            heat[pl.ds(wanted[j, c] + 7, 1), :] = arrived[pl.ds(j * cap + c, 1), :]
        return carry

    lax.fori_loop(0, n, land, 0)
    step = 64

    def solve(b, carry):
        at = pl.ds(pl.multiple_of(b * step, 8), step)
        k = conduct[at, :]
        left = 0.5 * (k + shifted(k, 1, 1, False))
        right = 0.5 * (k + shifted(k, -1, 1, False))
        lane = lax.broadcasted_iota(jnp.int32, k.shape, 1)
        left = jnp.where(lane == 0, 0.0, left)
        right = jnp.where(lane == k.shape[1] - 1, 0.0, right)
        cap_here = heat_cap[at, :]
        total = cap_here + left + right
        old = temp_old[at, :]
        target = cap_here * old + heat[pl.ds(pl.multiple_of(b * step + 8, 8), step), :] * factor
        current = old
        for _ in range(JACOBI):
            before = shifted(current, 1, 1, True)
            after = shifted(current, -1, 1, True)
            current = (target + left * before + right * after) / total
        temp_new[at, :] = current
        return carry

    lax.fori_loop(0, count // step, solve, 0)


def per_device(source, sigma_ref, owner, slot, temp_old, heat_cap, conduct):
    layers, blks = lax.axis_size("layer"), lax.axis_size("blk")
    peers = layers * blks
    ca, cr, lanes = source.shape
    count = temp_old.shape[0]
    positions, slot_code, block_code = routing(owner, slot, peers)
    cap = slot_code.shape[1]
    ask = jnp.pad(slot_code, ((0, 0), (0, 128 - cap)))[:, None, :]
    ext = pltpu.VMEM((ca + 2 * WIDE, cr + 2 * ROWS, lanes), jnp.float32)
    vmem, smem = pl.BlockSpec(memory_space=pltpu.VMEM), pl.BlockSpec(memory_space=pltpu.SMEM)
    each = pltpu.SemaphoreType.DMA((peers,))

    def kernel(*refs):
        exchange_kernel(layers, blks, ca, *refs)

    potential, arrived, wanted, sums = pl.pallas_call(
        kernel,
        out_shape=(
            jax.ShapeDtypeStruct(source.shape, jnp.float32),
            jax.ShapeDtypeStruct((peers * cap, lanes), jnp.float32),
            jax.ShapeDtypeStruct((peers, 1, 128), jnp.int32),
            jax.ShapeDtypeStruct((peers, 1, lanes), jnp.float32),
        ),
        in_specs=[vmem] * 4 + [smem] * 2,
        out_specs=(vmem,) * 4,
        scratch_shapes=[
            pltpu.SMEM((peers, 1, 128), jnp.int32),
            pltpu.VMEM((peers * cap, lanes), jnp.float32),
            pltpu.VMEM((peers * cap, lanes), jnp.float32),
            ext, ext, ext, ext, ext, ext, ext,
            pltpu.VMEM((ca * cr, lanes), jnp.float32),
            pltpu.VMEM((1, lanes), jnp.float32),
            pltpu.SemaphoreType.DMA((3,)),
            each, each, each, each, each, each, each, each,
            pltpu.SemaphoreType.DMA((2, 8)),
            pltpu.SemaphoreType.DMA((2, 8)),
        ],
        compiler_params=pltpu.CompilerParams(
            collective_id=0, has_side_effects=True, vmem_limit_bytes=40 << 20
        ),
    )(source, sigma_ref, temp_old, ask, positions.reshape(ca, cr), block_code)
    scale = source.size * peers

    def heat_step(*refs):
        thermal_kernel(float(scale), *refs)

    temp_new = pl.pallas_call(
        heat_step,
        out_shape=jax.ShapeDtypeStruct(temp_old.shape, jnp.float32),
        in_specs=[smem] + [vmem] * 5,
        out_specs=vmem,
        scratch_shapes=[pltpu.VMEM((count + 8, lanes), jnp.float32)],
        compiler_params=pltpu.CompilerParams(vmem_limit_bytes=40 << 20),
    )(wanted[:, 0, :cap], arrived, sums, temp_old, heat_cap, conduct)
    return (potential, temp_new)


def solution(mesh):
    return jax.shard_map(
        per_device,
        mesh=mesh,
        in_specs=(
            P("layer", "blk", None),
            P("layer", "blk", None),
            P("layer", "blk"),
            P("layer", "blk"),
            P(("blk", "layer"), None),
            P(("blk", "layer"), None),
            P(("blk", "layer"), None),
        ),
        out_specs=(P("layer", "blk", None), P(("blk", "layer"), None)),
        check_vma=False,
    )
```

```python
import jax
import jax.numpy as jnp
from jax import lax
from jax.experimental import pallas as pl
from jax.experimental.pallas import tpu as pltpu
from jax.sharding import PartitionSpec as P

SWEEPS = 3
JACOBI = 2


COUPLE = 0.4
THETA = 1.125
DELTA = 0.875


def routing(owner, slot, peers):
    owners = owner.reshape(-1)
    slots = slot.reshape(-1)
    count = owners.shape[0]
    capacity = 2 * count // peers
    named = owners[:, None] == jnp.arange(peers, dtype=jnp.int32)[None, :]
    named_bf = named.astype(jnp.bfloat16)
    order = jnp.arange(count, dtype=jnp.int32)
    earlier = (order[None, :] < order[:, None]).astype(jnp.bfloat16)
    before = jnp.dot(earlier, named_bf, preferred_element_type=jnp.float32)
    within = jnp.sum(jnp.where(named, before, 0.0), axis=1).astype(jnp.int32)
    here = within[:, None] == jnp.arange(capacity, dtype=jnp.int32)[None, :]
    parts = []
    for code in (slots + 1, order + 1):
        for digit in (code >> 5, code & 31):
            parts.append(jnp.where(here, digit[:, None].astype(jnp.float32), 0.0))
    table = jnp.concatenate(parts, axis=1).astype(jnp.bfloat16)
    digits = lax.dot_general(
        named_bf, table, (((0,), (0,)), ((), ())), preferred_element_type=jnp.float32
    ).astype(jnp.int32).reshape(peers, 4, capacity)
    slot_code = digits[:, 0] * 32 + digits[:, 1]
    block_code = digits[:, 2] * 32 + digits[:, 3]
    return owners * capacity + within, slot_code, block_code


WIDE = 4
ROWS = 8
MESH = pl.DeviceIdType.MESH


def shifted(x, step, axis, bounded):
    size = x.shape[axis]
    moved = pltpu.roll(x, step % size, axis)
    if bounded:
        place = lax.broadcasted_iota(jnp.int32, x.shape, axis)
        moved = jnp.where(place == (0 if step > 0 else size - 1), 0.0, moved)
    return moved


def around(ref, e):
    here = ref[e]
    return here, [
        ref[e + 1],
        ref[e - 1],
        shifted(here, -1, 0, False),
        shifted(here, 1, 0, False),
        shifted(here, -1, 1, True),
        shifted(here, 1, 1, True),
    ]


def exchange_kernel(
    layers, blks, slabs,
    source, sigma, temp_old, ask, places, blocks,
    potential, arrived, wanted, sums,
    asked, rows, fetched, src, cond, inv, dir_a, dir_b, res, pot, power, part,
    local_sem, ask_send, ask_recv, row_send, row_recv, pow_send, pow_recv, sum_send, sum_recv,
    halo_send, halo_recv,
):
    n = layers * blks
    cap = blocks.shape[1]
    ca, cr, lanes = source.shape
    blk, layer = lax.axis_index("blk"), lax.axis_index("layer")
    me = blk * layers + layer

    def wrap(x, size):
        return jnp.where(x >= size, x - size, jnp.where(x < 0, x + size, x))

    def others(body, sign):
        def outer(kl, carry):
            to_layer = wrap(layer + sign * kl, layers)

            def inner(pair, carry):
                for start in (blks // 2, 0):
                    to_blk = wrap(blk + sign * (pair + start), blks)
                    j = to_blk * layers + to_layer

                    def go(to_blk=to_blk, j=j):
                        body((to_blk, to_layer), j)

                    if start:
                        go()
                    else:
                        pl.when(jnp.logical_or(pair > 0, kl > 0))(go)
                return carry

            return lax.fori_loop(0, blks // 2, inner, carry)

        lax.fori_loop(0, layers, outer, 0)

    barrier = pltpu.get_barrier_semaphore()

    def greet(at, j):
        pl.semaphore_signal(barrier, inc=1, device_id=at, device_id_type=MESH)

    others(greet, 1)
    own_src = pltpu.make_async_copy(
        source, src.at[pl.ds(WIDE, ca), pl.ds(ROWS, cr)], local_sem.at[0]
    )
    own_src.start()
    own_ask = pltpu.make_async_copy(ask.at[me], wanted.at[me], local_sem.at[1])
    own_ask.start()
    pl.semaphore_wait(barrier, n - 1)

    def remote(src_ref, dst_ref, send, recv, at):
        return pltpu.make_async_remote_copy(
            src_ref=src_ref, dst_ref=dst_ref, send_sem=send, recv_sem=recv,
            device_id=at, device_id_type=MESH,
        )

    def ask_copy(at, j, slot):
        return remote(ask.at[j], wanted.at[slot], ask_send.at[j], ask_recv.at[slot], at)

    others(lambda at, j: ask_copy(at, j, me).start(), -1)

    directions = [(a, r) for a in (-1, 0, 1) for r in (-1, 0, 1) if (a, r) != (0, 0)]

    def halo(kind, d, field, whole):
        step_a, step_r = directions[d]
        count_a = ca if step_a == 0 else WIDE
        count_r = cr if step_r == 0 else ROWS
        from_a = ca - WIDE if step_a > 0 else 0
        from_r = cr - ROWS if step_r > 0 else 0
        to_a = {0: WIDE, 1: 0, -1: WIDE + ca}[step_a]
        to_r = {0: ROWS, 1: 0, -1: ROWS + cr}[step_r]
        off_a, off_r = (0, 0) if whole is not None else (WIDE, ROWS)
        origin = field if whole is None else whole
        return pltpu.make_async_remote_copy(
            src_ref=origin.at[pl.ds(off_a + from_a, count_a), pl.ds(off_r + from_r, count_r)],
            dst_ref=field.at[pl.ds(to_a, count_a), pl.ds(to_r, count_r)],
            send_sem=halo_send.at[kind, d],
            recv_sem=halo_recv.at[kind, d],
            device_id=(lax.rem(blk + step_r + blks, blks), lax.rem(layer + step_a + layers, layers)),
            device_id_type=MESH,
        )

    def halo_all(kind, field, whole, begin):
        for d, (step_a, _) in enumerate(directions):
            def act(d=d, incoming=False):
                copy = halo(kind, d, field, whole)
                if begin:
                    copy.start()
                elif incoming:
                    copy.wait_recv()
                else:
                    copy.wait_send()

            goes = {0: None, 1: layer < layers - 1, -1: layer > 0}[step_a]
            comes = {0: None, 1: layer > 0, -1: layer < layers - 1}[step_a]
            for cond_here, incoming in ((goes, False), (comes, True)):
                if begin and incoming:
                    continue
                if cond_here is None:
                    act(d, incoming)
                else:
                    pl.when(cond_here)(lambda d=d, incoming=incoming: act(d, incoming))

    halo_all(0, src, source, True)
    own_ask.wait()

    def row_copy(at, j, slot):
        return remote(
            rows.at[pl.ds(pl.multiple_of(j * cap, 8), cap)],
            fetched.at[pl.ds(pl.multiple_of(slot * cap, 8), cap)],
            row_send.at[j], row_recv.at[slot], at,
        )

    def fill(target, base, table, get):
        for c in range(cap):
            target[pl.ds(base + c, 1), :] = get(jnp.maximum(table(c) - 1, 0))

    others(lambda at, j: ask_copy(at, j, j).wait_recv(), 1)
    to_scalar = pltpu.make_async_copy(wanted, asked, local_sem.at[2])
    to_scalar.start()
    to_scalar.wait()

    def old_row(i):
        return temp_old[pl.ds(i, 1), :]

    def reply(at, j):
        fill(rows, pl.multiple_of(j * cap, 8), lambda c: asked[j, 0, c], old_row)
        row_copy(at, j, me).start()

    others(reply, 1)
    fill(fetched, pl.multiple_of(me * cap, 8), lambda c: asked[me, 0, c], old_row)
    others(lambda at, j: row_copy(at, j, j).wait_recv(), -1)

    def place(a, carry):
        for r in range(cr):
            cond[WIDE + a, pl.ds(ROWS + r, 1), :] = fetched[pl.ds(places[a, r], 1), :]
        here = cond[WIDE + a, pl.ds(ROWS, cr), :]
        cond[WIDE + a, pl.ds(ROWS, cr), :] = sigma[a] / (1.0 + COUPLE * here)
        return carry

    lax.fori_loop(0, ca, place, 0)
    halo_all(1, cond, None, True)

    @pl.when(layer == 0)
    def _():
        cond[0:WIDE] = jnp.zeros((WIDE, cr + 2 * ROWS, lanes), jnp.float32)

    @pl.when(layer == layers - 1)
    def _():
        cond[WIDE + ca :] = jnp.zeros((WIDE, cr + 2 * ROWS, lanes), jnp.float32)

    own_src.wait()
    halo_all(0, src, source, False)
    halo_all(1, cond, None, False)

    def inside(e, values):
        at = layer * ca + e - WIDE
        return jnp.where(jnp.logical_and(at >= 0, at < layers * ca), values, 0.0)

    ratio = THETA / DELTA
    rho = [1.0 / ratio]
    for _ in range(2):
        rho.append(1.0 / (2.0 * ratio - rho[-1]))

    def first(e, carry):
        here, others = around(cond, e)
        diag = 0.5 * (here + others[0])
        for other in others[1:]:
            diag = diag + 0.5 * (here + other)
        inverse = 1.0 / diag
        inv[e] = inverse
        dir_a[e] = inside(e, inverse * src[e] / THETA)
        return carry

    lax.fori_loop(1, 2 * WIDE + ca - 1, first, 0)

    def operate(field, e):
        here, others = around(cond, e)
        v, vs = around(field, e)
        result = 0.5 * (here + others[0]) * (v - vs[0])
        for other, other_v in zip(others[1:], vs[1:]):
            result = result + 0.5 * (here + other) * (v - other_v)
        return v, result

    def second(e, carry):
        v, applied = operate(dir_a, e)
        left = src[e] - applied
        res[e] = left
        step = inside(e, (rho[1] * rho[0]) * v + (2.0 * rho[1] / DELTA) * (inv[e] * left))
        dir_b[e] = step
        pot[e] = v + step
        return carry

    lax.fori_loop(2, 2 * WIDE + ca - 2, second, 0)

    def third(e, carry):
        v, applied = operate(dir_b, e)
        left = res[e] - applied
        step = inside(e, (rho[2] * rho[1]) * v + (2.0 * rho[2] / DELTA) * (inv[e] * left))
        pot[e] = pot[e] + step
        return carry

    lax.fori_loop(3, 2 * WIDE + ca - 3, third, 0)

    def joule(a, total):
        v, others = around(pot, a + WIDE)
        result = jnp.zeros_like(v)
        for other in others:
            gap = v - other
            result = result + 0.5 * gap * gap
        result = cond[a + WIDE] * result
        power[pl.ds(pl.multiple_of(a * cr, 8), cr), :] = result[ROWS : ROWS + cr]
        potential[a] = v[ROWS : ROWS + cr]
        return total + jnp.sum(result[ROWS : ROWS + cr], axis=0, keepdims=True)

    part[...] = lax.fori_loop(0, ca, joule, jnp.zeros((1, lanes), jnp.float32))
    sums[me] = part[...]

    def pow_copy(at, j, slot):
        return remote(
            rows.at[pl.ds(pl.multiple_of(j * cap, 8), cap)],
            arrived.at[pl.ds(pl.multiple_of(slot * cap, 8), cap)],
            pow_send.at[j], pow_recv.at[slot], at,
        )

    def sum_copy(at, j, slot):
        return remote(part, sums.at[slot], sum_send.at[j], sum_recv.at[slot], at)

    def power_row(i):
        return power[pl.ds(i, 1), :]

    def send_power(at, j):
        row_copy(at, j, me).wait_send()
        fill(rows, pl.multiple_of(j * cap, 8), lambda c: blocks[j, c], power_row)
        pow_copy(at, j, me).start()
        sum_copy(at, j, me).start()

    others(send_power, 1)
    fill(arrived, pl.multiple_of(me * cap, 8), lambda c: blocks[me, c], power_row)

    def finish(at, j):
        ask_copy(at, j, j).wait_send()
        pow_copy(at, j, j).wait()
        sum_copy(at, j, j).wait()

    others(finish, -1)


def thermal_kernel(
    scale, wanted, potential_in, arrived, sums, temp_old, heat_cap, conduct,
    temp_new, potential, heat, sem,
):
    through = pltpu.make_async_copy(potential_in, potential, sem)
    through.start()
    n, cap = wanted.shape
    count = temp_old.shape[0]
    factor = scale / jnp.sum(sums[...])

    def land(j, carry):
        for group in range(0, cap, 8):
            @pl.when(wanted[j, group] > 0)
            def _(group=group):
                for c in range(group, group + 8):
                    heat[pl.ds(wanted[j, c] + 7, 1), :] = arrived[pl.ds(j * cap + c, 1), :]

        return carry

    lax.fori_loop(0, n, land, 0)
    step = 64

    def solve(b, carry):
        at = pl.ds(pl.multiple_of(b * step, 8), step)
        k = conduct[at, :]
        left = 0.5 * (k + shifted(k, 1, 1, False))
        right = 0.5 * (k + shifted(k, -1, 1, False))
        lane = lax.broadcasted_iota(jnp.int32, k.shape, 1)
        left = jnp.where(lane == 0, 0.0, left)
        right = jnp.where(lane == k.shape[1] - 1, 0.0, right)
        cap_here = heat_cap[at, :]
        total = cap_here + left + right
        old = temp_old[at, :]
        target = cap_here * old + heat[pl.ds(pl.multiple_of(b * step + 8, 8), step), :] * factor
        current = old
        for _ in range(JACOBI):
            before = shifted(current, 1, 1, True)
            after = shifted(current, -1, 1, True)
            current = (target + left * before + right * after) / total
        temp_new[at, :] = current
        return carry

    lax.fori_loop(0, count // step, solve, 0)
    through.wait()


def per_device(source, sigma_ref, owner, slot, temp_old, heat_cap, conduct):
    layers, blks = lax.axis_size("layer"), lax.axis_size("blk")
    peers = layers * blks
    ca, cr, lanes = source.shape
    count = temp_old.shape[0]
    positions, slot_code, block_code = routing(owner, slot, peers)
    cap = slot_code.shape[1]
    ask = jnp.pad(slot_code, ((0, 0), (0, 128 - cap)))[:, None, :]
    ext = pltpu.VMEM((ca + 2 * WIDE, cr + 2 * ROWS, lanes), jnp.float32)
    vmem, smem = pl.BlockSpec(memory_space=pltpu.VMEM), pl.BlockSpec(memory_space=pltpu.SMEM)
    each = pltpu.SemaphoreType.DMA((peers,))

    def kernel(*refs):
        exchange_kernel(layers, blks, ca, *refs)

    potential, arrived, wanted, sums = pl.pallas_call(
        kernel,
        out_shape=(
            jax.ShapeDtypeStruct(source.shape, jnp.float32),
            jax.ShapeDtypeStruct((peers * cap, lanes), jnp.float32),
            jax.ShapeDtypeStruct((peers, 1, 128), jnp.int32),
            jax.ShapeDtypeStruct((peers, 1, lanes), jnp.float32),
        ),
        in_specs=[vmem] * 4 + [smem] * 2,
        out_specs=(vmem,) * 4,
        scratch_shapes=[
            pltpu.SMEM((peers, 1, 128), jnp.int32),
            pltpu.VMEM((peers * cap, lanes), jnp.float32),
            pltpu.VMEM((peers * cap, lanes), jnp.float32),
            ext, ext, ext, ext, ext, ext, ext,
            pltpu.VMEM((ca * cr, lanes), jnp.float32),
            pltpu.VMEM((1, lanes), jnp.float32),
            pltpu.SemaphoreType.DMA((3,)),
            each, each, each, each, each, each, each, each,
            pltpu.SemaphoreType.DMA((2, 8)),
            pltpu.SemaphoreType.DMA((2, 8)),
        ],
        compiler_params=pltpu.CompilerParams(
            collective_id=0, has_side_effects=True, vmem_limit_bytes=40 << 20
        ),
    )(source, sigma_ref, temp_old, ask, positions.reshape(ca, cr), block_code)
    scale = source.size * peers

    def heat_step(*refs):
        thermal_kernel(float(scale), *refs)

    whole = pl.BlockSpec(memory_space=pl.ANY)
    temp_new, potential = pl.pallas_call(
        heat_step,
        out_shape=(
            jax.ShapeDtypeStruct(temp_old.shape, jnp.float32),
            jax.ShapeDtypeStruct(source.shape, jnp.float32),
        ),
        in_specs=[smem, whole] + [vmem] * 5,
        out_specs=(vmem, whole),
        scratch_shapes=[
            pltpu.VMEM((count + 8, lanes), jnp.float32),
            pltpu.SemaphoreType.DMA(()),
        ],
        compiler_params=pltpu.CompilerParams(vmem_limit_bytes=40 << 20),
    )(wanted[:, 0, :cap], potential, arrived, sums, temp_old, heat_cap, conduct)
    return (potential, temp_new)


def solution(mesh):
    return jax.shard_map(
        per_device,
        mesh=mesh,
        in_specs=(
            P("layer", "blk", None),
            P("layer", "blk", None),
            P("layer", "blk"),
            P("layer", "blk"),
            P(("blk", "layer"), None),
            P(("blk", "layer"), None),
            P(("blk", "layer"), None),
        ),
        out_specs=(P("layer", "blk", None), P(("blk", "layer"), None)),
        check_vma=False,
    )
```

```python
import jax
import jax.numpy as jnp
from jax import lax
from jax.experimental import pallas as pl
from jax.experimental.pallas import tpu as pltpu
from jax.sharding import PartitionSpec as P

SWEEPS = 3
JACOBI = 2


COUPLE = 0.4
THETA = 1.125
DELTA = 0.875


def routing(owner, slot, peers):
    owners = owner.reshape(-1)
    slots = slot.reshape(-1)
    count = owners.shape[0]
    capacity = 2 * count // peers
    named = owners[:, None] == jnp.arange(peers, dtype=jnp.int32)[None, :]
    named_bf = named.astype(jnp.bfloat16)
    order = jnp.arange(count, dtype=jnp.int32)
    earlier = (order[None, :] < order[:, None]).astype(jnp.bfloat16)
    before = jnp.dot(earlier, named_bf, preferred_element_type=jnp.float32)
    within = jnp.sum(jnp.where(named, before, 0.0), axis=1).astype(jnp.int32)
    here = within[:, None] == jnp.arange(capacity, dtype=jnp.int32)[None, :]
    parts = []
    for code in (slots + 1, order + 1):
        for digit in (code >> 5, code & 31):
            parts.append(jnp.where(here, digit[:, None].astype(jnp.float32), 0.0))
    table = jnp.concatenate(parts, axis=1).astype(jnp.bfloat16)
    digits = lax.dot_general(
        named_bf, table, (((0,), (0,)), ((), ())), preferred_element_type=jnp.float32
    ).astype(jnp.int32).reshape(peers, 4, capacity)
    slot_code = digits[:, 0] * 32 + digits[:, 1]
    block_code = digits[:, 2] * 32 + digits[:, 3]
    return owners * capacity + within, slot_code, block_code


WIDE = 4
ROWS = 8
MESH = pl.DeviceIdType.MESH


def shifted(x, step, axis, bounded):
    size = x.shape[axis]
    moved = pltpu.roll(x, step % size, axis)
    if bounded:
        place = lax.broadcasted_iota(jnp.int32, x.shape, axis)
        moved = jnp.where(place == (0 if step > 0 else size - 1), 0.0, moved)
    return moved


def around(ref, e):
    here = ref[e]
    return here, [
        ref[e + 1],
        ref[e - 1],
        shifted(here, -1, 0, False),
        shifted(here, 1, 0, False),
        shifted(here, -1, 1, True),
        shifted(here, 1, 1, True),
    ]


def exchange_kernel(
    layers, blks, slabs,
    source, sigma, temp_old, ask, places, blocks,
    potential, arrived, wanted, sums,
    asked, rows, fetched, src, cond, inv, dir_a, dir_b, res, pot, power, part,
    local_sem, ask_send, ask_recv, row_send, row_recv, pow_send, pow_recv, sum_send, sum_recv,
    halo_send, halo_recv,
):
    n = layers * blks
    cap = blocks.shape[1]
    ca, cr, lanes = source.shape
    blk, layer = lax.axis_index("blk"), lax.axis_index("layer")
    me = blk * layers + layer

    def wrap(x, size):
        return jnp.where(x >= size, x - size, jnp.where(x < 0, x + size, x))

    def others(body, sign):
        def outer(kl, carry):
            to_layer = wrap(layer + sign * kl, layers)

            def inner(pair, carry):
                for start in (blks // 2, 0):
                    to_blk = wrap(blk + sign * (pair + start), blks)
                    j = to_blk * layers + to_layer

                    def go(to_blk=to_blk, j=j):
                        body((to_blk, to_layer), j)

                    if start:
                        go()
                    else:
                        pl.when(jnp.logical_or(pair > 0, kl > 0))(go)
                return carry

            return lax.fori_loop(0, blks // 2, inner, carry)

        lax.fori_loop(0, layers, outer, 0)

    barrier = pltpu.get_barrier_semaphore()

    def greet(at, j):
        pl.semaphore_signal(barrier, inc=1, device_id=at, device_id_type=MESH)

    others(greet, 1)
    own_src = pltpu.make_async_copy(
        source, src.at[pl.ds(WIDE, ca), pl.ds(ROWS, cr)], local_sem.at[0]
    )
    own_src.start()
    own_ask = pltpu.make_async_copy(ask.at[me], wanted.at[me], local_sem.at[1])
    own_ask.start()
    pl.semaphore_wait(barrier, n - 1)

    def remote(src_ref, dst_ref, send, recv, at):
        return pltpu.make_async_remote_copy(
            src_ref=src_ref, dst_ref=dst_ref, send_sem=send, recv_sem=recv,
            device_id=at, device_id_type=MESH,
        )

    def ask_copy(at, j, slot):
        return remote(ask.at[j], wanted.at[slot], ask_send.at[j], ask_recv.at[slot], at)

    others(lambda at, j: ask_copy(at, j, me).start(), -1)

    directions = [(a, r) for a in (-1, 0, 1) for r in (-1, 0, 1) if (a, r) != (0, 0)]

    def halo(kind, d, field, whole):
        step_a, step_r = directions[d]
        count_a = ca if step_a == 0 else WIDE
        count_r = cr if step_r == 0 else ROWS
        from_a = ca - WIDE if step_a > 0 else 0
        from_r = cr - ROWS if step_r > 0 else 0
        to_a = {0: WIDE, 1: 0, -1: WIDE + ca}[step_a]
        to_r = {0: ROWS, 1: 0, -1: ROWS + cr}[step_r]
        off_a, off_r = (0, 0) if whole is not None else (WIDE, ROWS)
        origin = field if whole is None else whole
        return pltpu.make_async_remote_copy(
            src_ref=origin.at[pl.ds(off_a + from_a, count_a), pl.ds(off_r + from_r, count_r)],
            dst_ref=field.at[pl.ds(to_a, count_a), pl.ds(to_r, count_r)],
            send_sem=halo_send.at[kind, d],
            recv_sem=halo_recv.at[kind, d],
            device_id=(lax.rem(blk + step_r + blks, blks), lax.rem(layer + step_a + layers, layers)),
            device_id_type=MESH,
        )

    def halo_all(kind, field, whole, begin):
        for d, (step_a, _) in enumerate(directions):
            def act(d=d, incoming=False):
                copy = halo(kind, d, field, whole)
                if begin:
                    copy.start()
                elif incoming:
                    copy.wait_recv()
                else:
                    copy.wait_send()

            goes = {0: None, 1: layer < layers - 1, -1: layer > 0}[step_a]
            comes = {0: None, 1: layer > 0, -1: layer < layers - 1}[step_a]
            for cond_here, incoming in ((goes, False), (comes, True)):
                if begin and incoming:
                    continue
                if cond_here is None:
                    act(d, incoming)
                else:
                    pl.when(cond_here)(lambda d=d, incoming=incoming: act(d, incoming))

    halo_all(0, src, source, True)
    own_ask.wait()

    def row_copy(at, j, slot):
        return remote(
            rows.at[pl.ds(pl.multiple_of(j * cap, 8), cap)],
            fetched.at[pl.ds(pl.multiple_of(slot * cap, 8), cap)],
            row_send.at[j], row_recv.at[slot], at,
        )

    def fill(target, base, table, get):
        for c in range(cap):
            target[pl.ds(base + c, 1), :] = get(jnp.maximum(table(c) - 1, 0))

    others(lambda at, j: ask_copy(at, j, j).wait_recv(), 1)
    to_scalar = pltpu.make_async_copy(wanted, asked, local_sem.at[2])
    to_scalar.start()
    to_scalar.wait()

    def old_row(i):
        return temp_old[pl.ds(i, 1), :]

    def reply(at, j):
        fill(rows, pl.multiple_of(j * cap, 8), lambda c: asked[j, 0, c], old_row)
        row_copy(at, j, me).start()

    others(reply, 1)
    fill(fetched, pl.multiple_of(me * cap, 8), lambda c: asked[me, 0, c], old_row)
    others(lambda at, j: row_copy(at, j, j).wait_recv(), -1)

    def place(a, carry):
        for r in range(cr):
            cond[WIDE + a, pl.ds(ROWS + r, 1), :] = fetched[pl.ds(places[a, r], 1), :]
        here = cond[WIDE + a, pl.ds(ROWS, cr), :]
        cond[WIDE + a, pl.ds(ROWS, cr), :] = sigma[a] / (1.0 + COUPLE * here)
        return carry

    lax.fori_loop(0, ca, place, 0)
    halo_all(1, cond, None, True)

    @pl.when(layer == 0)
    def _():
        cond[0:WIDE] = jnp.zeros((WIDE, cr + 2 * ROWS, lanes), jnp.float32)

    @pl.when(layer == layers - 1)
    def _():
        cond[WIDE + ca :] = jnp.zeros((WIDE, cr + 2 * ROWS, lanes), jnp.float32)

    own_src.wait()
    halo_all(0, src, source, False)
    halo_all(1, cond, None, False)

    def inside(e, values):
        at = layer * ca + e - WIDE
        return jnp.where(jnp.logical_and(at >= 0, at < layers * ca), values, 0.0)

    ratio = THETA / DELTA
    rho = [1.0 / ratio]
    for _ in range(2):
        rho.append(1.0 / (2.0 * ratio - rho[-1]))

    def first(e, carry):
        here, others = around(cond, e)
        diag = 0.5 * (here + others[0])
        for other in others[1:]:
            diag = diag + 0.5 * (here + other)
        inverse = 1.0 / diag
        inv[e] = inverse
        dir_a[e] = inside(e, inverse * src[e] / THETA)
        return carry

    lax.fori_loop(1, 2 * WIDE + ca - 1, first, 0, unroll=2)

    def operate(field, e):
        here, others = around(cond, e)
        v, vs = around(field, e)
        result = 0.5 * (here + others[0]) * (v - vs[0])
        for other, other_v in zip(others[1:], vs[1:]):
            result = result + 0.5 * (here + other) * (v - other_v)
        return v, result

    def second(e, carry):
        v, applied = operate(dir_a, e)
        left = src[e] - applied
        res[e] = left
        step = inside(e, (rho[1] * rho[0]) * v + (2.0 * rho[1] / DELTA) * (inv[e] * left))
        dir_b[e] = step
        pot[e] = v + step
        return carry

    lax.fori_loop(2, 2 * WIDE + ca - 2, second, 0, unroll=2)

    def third(e, carry):
        v, applied = operate(dir_b, e)
        left = res[e] - applied
        step = inside(e, (rho[2] * rho[1]) * v + (2.0 * rho[2] / DELTA) * (inv[e] * left))
        pot[e] = pot[e] + step
        return carry

    lax.fori_loop(3, 2 * WIDE + ca - 3, third, 0, unroll=2)

    def joule(a, total):
        v, others = around(pot, a + WIDE)
        result = jnp.zeros_like(v)
        for other in others:
            gap = v - other
            result = result + 0.5 * gap * gap
        result = cond[a + WIDE] * result
        power[pl.ds(pl.multiple_of(a * cr, 8), cr), :] = result[ROWS : ROWS + cr]
        potential[a] = v[ROWS : ROWS + cr]
        return total + jnp.sum(result[ROWS : ROWS + cr], axis=0, keepdims=True)

    part[...] = lax.fori_loop(0, ca, joule, jnp.zeros((1, lanes), jnp.float32))
    sums[me] = part[...]

    def pow_copy(at, j, slot):
        return remote(
            rows.at[pl.ds(pl.multiple_of(j * cap, 8), cap)],
            arrived.at[pl.ds(pl.multiple_of(slot * cap, 8), cap)],
            pow_send.at[j], pow_recv.at[slot], at,
        )

    def sum_copy(at, j, slot):
        return remote(part, sums.at[slot], sum_send.at[j], sum_recv.at[slot], at)

    def power_row(i):
        return power[pl.ds(i, 1), :]

    def send_power(at, j):
        row_copy(at, j, me).wait_send()
        fill(rows, pl.multiple_of(j * cap, 8), lambda c: blocks[j, c], power_row)
        pow_copy(at, j, me).start()
        sum_copy(at, j, me).start()

    others(send_power, 1)
    fill(arrived, pl.multiple_of(me * cap, 8), lambda c: blocks[me, c], power_row)

    def finish(at, j):
        ask_copy(at, j, j).wait_send()
        pow_copy(at, j, j).wait()
        sum_copy(at, j, j).wait()

    others(finish, -1)


def thermal_kernel(
    scale, wanted, potential_in, arrived, sums, temp_old, heat_cap, conduct,
    temp_new, potential, heat, sem,
):
    through = pltpu.make_async_copy(potential_in, potential, sem)
    through.start()
    n, cap = wanted.shape
    count = temp_old.shape[0]
    factor = scale / jnp.sum(sums[...])

    def land(j, carry):
        for c in range(cap):
            heat[pl.ds(wanted[j, c] + 7, 1), :] = arrived[pl.ds(j * cap + c, 1), :]
        return carry

    lax.fori_loop(0, n, land, 0)
    step = 128

    def solve(b, carry):
        at = pl.ds(pl.multiple_of(b * step, 8), step)
        k = conduct[at, :]
        left = 0.5 * (k + shifted(k, 1, 1, False))
        right = 0.5 * (k + shifted(k, -1, 1, False))
        lane = lax.broadcasted_iota(jnp.int32, k.shape, 1)
        left = jnp.where(lane == 0, 0.0, left)
        right = jnp.where(lane == k.shape[1] - 1, 0.0, right)
        cap_here = heat_cap[at, :]
        total = cap_here + left + right
        old = temp_old[at, :]
        target = cap_here * old + heat[pl.ds(pl.multiple_of(b * step + 8, 8), step), :] * factor
        current = old
        for _ in range(JACOBI):
            before = shifted(current, 1, 1, True)
            after = shifted(current, -1, 1, True)
            current = (target + left * before + right * after) / total
        temp_new[at, :] = current
        return carry

    lax.fori_loop(0, count // step, solve, 0)
    through.wait()


def per_device(source, sigma_ref, owner, slot, temp_old, heat_cap, conduct):
    layers, blks = lax.axis_size("layer"), lax.axis_size("blk")
    peers = layers * blks
    ca, cr, lanes = source.shape
    count = temp_old.shape[0]
    positions, slot_code, block_code = routing(owner, slot, peers)
    cap = slot_code.shape[1]
    ask = jnp.pad(slot_code, ((0, 0), (0, 128 - cap)))[:, None, :]
    ext = pltpu.VMEM((ca + 2 * WIDE, cr + 2 * ROWS, lanes), jnp.float32)
    vmem, smem = pl.BlockSpec(memory_space=pltpu.VMEM), pl.BlockSpec(memory_space=pltpu.SMEM)
    each = pltpu.SemaphoreType.DMA((peers,))

    def kernel(*refs):
        exchange_kernel(layers, blks, ca, *refs)

    potential, arrived, wanted, sums = pl.pallas_call(
        kernel,
        out_shape=(
            jax.ShapeDtypeStruct(source.shape, jnp.float32),
            jax.ShapeDtypeStruct((peers * cap, lanes), jnp.float32),
            jax.ShapeDtypeStruct((peers, 1, 128), jnp.int32),
            jax.ShapeDtypeStruct((peers, 1, lanes), jnp.float32),
        ),
        in_specs=[vmem] * 4 + [smem] * 2,
        out_specs=(vmem,) * 4,
        scratch_shapes=[
            pltpu.SMEM((peers, 1, 128), jnp.int32),
            pltpu.VMEM((peers * cap, lanes), jnp.float32),
            pltpu.VMEM((peers * cap, lanes), jnp.float32),
            ext, ext, ext, ext, ext, ext, ext,
            pltpu.VMEM((ca * cr, lanes), jnp.float32),
            pltpu.VMEM((1, lanes), jnp.float32),
            pltpu.SemaphoreType.DMA((3,)),
            each, each, each, each, each, each, each, each,
            pltpu.SemaphoreType.DMA((2, 8)),
            pltpu.SemaphoreType.DMA((2, 8)),
        ],
        compiler_params=pltpu.CompilerParams(
            collective_id=0, has_side_effects=True, vmem_limit_bytes=40 << 20
        ),
    )(source, sigma_ref, temp_old, ask, positions.reshape(ca, cr), block_code)
    scale = source.size * peers

    def heat_step(*refs):
        thermal_kernel(float(scale), *refs)

    whole = pl.BlockSpec(memory_space=pl.ANY)
    temp_new, potential = pl.pallas_call(
        heat_step,
        out_shape=(
            jax.ShapeDtypeStruct(temp_old.shape, jnp.float32),
            jax.ShapeDtypeStruct(source.shape, jnp.float32),
        ),
        in_specs=[smem, whole] + [vmem] * 5,
        out_specs=(vmem, whole),
        scratch_shapes=[
            pltpu.VMEM((count + 8, lanes), jnp.float32),
            pltpu.SemaphoreType.DMA(()),
        ],
        compiler_params=pltpu.CompilerParams(vmem_limit_bytes=40 << 20),
    )(wanted[:, 0, :cap], potential, arrived, sums, temp_old, heat_cap, conduct)
    return (potential, temp_new)


def solution(mesh):
    return jax.shard_map(
        per_device,
        mesh=mesh,
        in_specs=(
            P("layer", "blk", None),
            P("layer", "blk", None),
            P("layer", "blk"),
            P("layer", "blk"),
            P(("blk", "layer"), None),
            P(("blk", "layer"), None),
            P(("blk", "layer"), None),
        ),
        out_specs=(P("layer", "blk", None), P(("blk", "layer"), None)),
        check_vma=False,
    )
```

```python
import jax
import jax.numpy as jnp
from jax import lax
from jax.experimental import pallas as pl
from jax.experimental.pallas import tpu as pltpu
from jax.sharding import PartitionSpec as P

SWEEPS = 3
JACOBI = 2


COUPLE = 0.4
THETA = 1.125
DELTA = 0.875


def routing(owner, slot, peers):
    owners = owner.reshape(-1)
    slots = slot.reshape(-1)
    count = owners.shape[0]
    capacity = 2 * count // peers
    named = owners[:, None] == jnp.arange(peers, dtype=jnp.int32)[None, :]
    named_bf = named.astype(jnp.bfloat16)
    order = jnp.arange(count, dtype=jnp.int32)
    earlier = (order[None, :] < order[:, None]).astype(jnp.bfloat16)
    before = jnp.dot(earlier, named_bf, preferred_element_type=jnp.float32)
    within = jnp.sum(jnp.where(named, before, 0.0), axis=1).astype(jnp.int32)
    here = within[:, None] == jnp.arange(capacity, dtype=jnp.int32)[None, :]
    parts = []
    for code in (slots + 1, order + 1):
        for digit in (code >> 5, code & 31):
            parts.append(jnp.where(here, digit[:, None].astype(jnp.float32), 0.0))
    table = jnp.concatenate(parts, axis=1).astype(jnp.bfloat16)
    digits = lax.dot_general(
        named_bf, table, (((0,), (0,)), ((), ())), preferred_element_type=jnp.float32
    ).astype(jnp.int32).reshape(peers, 4, capacity)
    slot_code = digits[:, 0] * 32 + digits[:, 1]
    block_code = digits[:, 2] * 32 + digits[:, 3]
    return owners * capacity + within, slot_code, block_code


WIDE = 4
ROWS = 8
MESH = pl.DeviceIdType.MESH


def shifted(x, step, axis, bounded):
    size = x.shape[axis]
    moved = pltpu.roll(x, step % size, axis)
    if bounded:
        place = lax.broadcasted_iota(jnp.int32, x.shape, axis)
        moved = jnp.where(place == (0 if step > 0 else size - 1), 0.0, moved)
    return moved


def around(ref, e):
    here = ref[e]
    return here, [
        ref[e + 1],
        ref[e - 1],
        shifted(here, -1, 0, False),
        shifted(here, 1, 0, False),
        shifted(here, -1, 1, True),
        shifted(here, 1, 1, True),
    ]


def exchange_kernel(
    layers, blks, slabs,
    source, sigma, temp_old, ask, places, blocks,
    potential, arrived, wanted, sums,
    asked, rows, fetched, src, cond, inv, dir_a, dir_b, res, pot, power, part,
    local_sem, ask_send, ask_recv, row_send, row_recv, pow_send, pow_recv, sum_send, sum_recv,
    halo_send, halo_recv,
):
    n = layers * blks
    cap = blocks.shape[1]
    ca, cr, lanes = source.shape
    blk, layer = lax.axis_index("blk"), lax.axis_index("layer")
    me = blk * layers + layer

    def wrap(x, size):
        return jnp.where(x >= size, x - size, jnp.where(x < 0, x + size, x))

    def others(body, sign):
        def outer(kl, carry):
            to_layer = wrap(layer + sign * kl, layers)

            def inner(pair, carry):
                for start in (blks // 2, 0):
                    to_blk = wrap(blk + sign * (pair + start), blks)
                    j = to_blk * layers + to_layer

                    def go(to_blk=to_blk, j=j):
                        body((to_blk, to_layer), j)

                    if start:
                        go()
                    else:
                        pl.when(jnp.logical_or(pair > 0, kl > 0))(go)
                return carry

            return lax.fori_loop(0, blks // 2, inner, carry)

        lax.fori_loop(0, layers, outer, 0)

    barrier = pltpu.get_barrier_semaphore()

    def greet(at, j):
        pl.semaphore_signal(barrier, inc=1, device_id=at, device_id_type=MESH)

    others(greet, 1)
    own_src = pltpu.make_async_copy(
        source, src.at[pl.ds(WIDE, ca), pl.ds(ROWS, cr)], local_sem.at[0]
    )
    own_src.start()
    own_ask = pltpu.make_async_copy(ask.at[me], wanted.at[me], local_sem.at[1])
    own_ask.start()
    pl.semaphore_wait(barrier, n - 1)

    def remote(src_ref, dst_ref, send, recv, at):
        return pltpu.make_async_remote_copy(
            src_ref=src_ref, dst_ref=dst_ref, send_sem=send, recv_sem=recv,
            device_id=at, device_id_type=MESH,
        )

    def ask_copy(at, j, slot):
        return remote(ask.at[j], wanted.at[slot], ask_send.at[j], ask_recv.at[slot], at)

    others(lambda at, j: ask_copy(at, j, me).start(), -1)

    directions = [(a, r) for a in (-1, 0, 1) for r in (-1, 0, 1) if (a, r) != (0, 0)]

    def halo(kind, d, field, whole):
        step_a, step_r = directions[d]
        count_a = ca if step_a == 0 else WIDE
        count_r = cr if step_r == 0 else ROWS
        from_a = ca - WIDE if step_a > 0 else 0
        from_r = cr - ROWS if step_r > 0 else 0
        to_a = {0: WIDE, 1: 0, -1: WIDE + ca}[step_a]
        to_r = {0: ROWS, 1: 0, -1: ROWS + cr}[step_r]
        off_a, off_r = (0, 0) if whole is not None else (WIDE, ROWS)
        origin = field if whole is None else whole
        return pltpu.make_async_remote_copy(
            src_ref=origin.at[pl.ds(off_a + from_a, count_a), pl.ds(off_r + from_r, count_r)],
            dst_ref=field.at[pl.ds(to_a, count_a), pl.ds(to_r, count_r)],
            send_sem=halo_send.at[kind, d],
            recv_sem=halo_recv.at[kind, d],
            device_id=(lax.rem(blk + step_r + blks, blks), lax.rem(layer + step_a + layers, layers)),
            device_id_type=MESH,
        )

    def halo_all(kind, field, whole, begin):
        for d, (step_a, _) in enumerate(directions):
            def act(d=d, incoming=False):
                copy = halo(kind, d, field, whole)
                if begin:
                    copy.start()
                elif incoming:
                    copy.wait_recv()
                else:
                    copy.wait_send()

            goes = {0: None, 1: layer < layers - 1, -1: layer > 0}[step_a]
            comes = {0: None, 1: layer > 0, -1: layer < layers - 1}[step_a]
            for cond_here, incoming in ((goes, False), (comes, True)):
                if begin and incoming:
                    continue
                if cond_here is None:
                    act(d, incoming)
                else:
                    pl.when(cond_here)(lambda d=d, incoming=incoming: act(d, incoming))

    halo_all(0, src, source, True)
    own_ask.wait()

    def row_copy(at, j, slot):
        return remote(
            rows.at[pl.ds(pl.multiple_of(j * cap, 8), cap)],
            fetched.at[pl.ds(pl.multiple_of(slot * cap, 8), cap)],
            row_send.at[j], row_recv.at[slot], at,
        )

    def fill(target, base, table, get):
        for c in range(cap):
            target[pl.ds(base + c, 1), :] = get(jnp.maximum(table(c) - 1, 0))

    others(lambda at, j: ask_copy(at, j, j).wait_recv(), 1)
    to_scalar = pltpu.make_async_copy(wanted, asked, local_sem.at[2])
    to_scalar.start()
    to_scalar.wait()

    def old_row(i):
        return temp_old[pl.ds(i, 1), :]

    def reply(at, j):
        fill(rows, pl.multiple_of(j * cap, 8), lambda c: asked[j, 0, c], old_row)
        row_copy(at, j, me).start()

    others(reply, 1)
    fill(fetched, pl.multiple_of(me * cap, 8), lambda c: asked[me, 0, c], old_row)
    others(lambda at, j: row_copy(at, j, j).wait_recv(), -1)

    def place(a, carry):
        for r in range(cr):
            cond[WIDE + a, pl.ds(ROWS + r, 1), :] = fetched[pl.ds(places[a, r], 1), :]
        here = cond[WIDE + a, pl.ds(ROWS, cr), :]
        cond[WIDE + a, pl.ds(ROWS, cr), :] = sigma[a] / (1.0 + COUPLE * here)
        return carry

    lax.fori_loop(0, ca, place, 0)
    halo_all(1, cond, None, True)

    @pl.when(layer == 0)
    def _():
        cond[0:WIDE] = jnp.zeros((WIDE, cr + 2 * ROWS, lanes), jnp.float32)

    @pl.when(layer == layers - 1)
    def _():
        cond[WIDE + ca :] = jnp.zeros((WIDE, cr + 2 * ROWS, lanes), jnp.float32)

    own_src.wait()
    halo_all(0, src, source, False)
    halo_all(1, cond, None, False)

    def inside(e, values):
        at = layer * ca + e - WIDE
        return jnp.where(jnp.logical_and(at >= 0, at < layers * ca), values, 0.0)

    ratio = THETA / DELTA
    rho = [1.0 / ratio]
    for _ in range(2):
        rho.append(1.0 / (2.0 * ratio - rho[-1]))

    def first(e, carry):
        here, others = around(cond, e)
        diag = 0.5 * (here + others[0])
        for other in others[1:]:
            diag = diag + 0.5 * (here + other)
        inverse = 1.0 / diag
        inv[e] = inverse
        dir_a[e] = inside(e, inverse * src[e] / THETA)
        return carry

    lax.fori_loop(1, 2 * WIDE + ca - 1, first, 0, unroll=2)

    def operate(field, e):
        here, others = around(cond, e)
        v, vs = around(field, e)
        result = 0.5 * (here + others[0]) * (v - vs[0])
        for other, other_v in zip(others[1:], vs[1:]):
            result = result + 0.5 * (here + other) * (v - other_v)
        return v, result

    def second(e, carry):
        v, applied = operate(dir_a, e)
        left = src[e] - applied
        res[e] = left
        step = inside(e, (rho[1] * rho[0]) * v + (2.0 * rho[1] / DELTA) * (inv[e] * left))
        dir_b[e] = step
        pot[e] = v + step
        return carry

    lax.fori_loop(2, 2 * WIDE + ca - 2, second, 0, unroll=4)

    def third(e, carry):
        v, applied = operate(dir_b, e)
        left = res[e] - applied
        step = inside(e, (rho[2] * rho[1]) * v + (2.0 * rho[2] / DELTA) * (inv[e] * left))
        pot[e] = pot[e] + step
        return carry

    lax.fori_loop(3, 2 * WIDE + ca - 3, third, 0, unroll=3)

    def joule(a, total):
        v, others = around(pot, a + WIDE)
        result = jnp.zeros_like(v)
        for other in others:
            gap = v - other
            result = result + 0.5 * gap * gap
        result = cond[a + WIDE] * result
        power[pl.ds(pl.multiple_of(a * cr, 8), cr), :] = result[ROWS : ROWS + cr]
        potential[a] = v[ROWS : ROWS + cr]
        return total + jnp.sum(result[ROWS : ROWS + cr], axis=0, keepdims=True)

    part[...] = lax.fori_loop(0, ca, joule, jnp.zeros((1, lanes), jnp.float32), unroll=2)
    sums[me] = part[...]

    def pow_copy(at, j, slot):
        return remote(
            rows.at[pl.ds(pl.multiple_of(j * cap, 8), cap)],
            arrived.at[pl.ds(pl.multiple_of(slot * cap, 8), cap)],
            pow_send.at[j], pow_recv.at[slot], at,
        )

    def sum_copy(at, j, slot):
        return remote(part, sums.at[slot], sum_send.at[j], sum_recv.at[slot], at)

    def power_row(i):
        return power[pl.ds(i, 1), :]

    def send_power(at, j):
        row_copy(at, j, me).wait_send()
        fill(rows, pl.multiple_of(j * cap, 8), lambda c: blocks[j, c], power_row)
        pow_copy(at, j, me).start()
        sum_copy(at, j, me).start()

    others(send_power, 1)
    fill(arrived, pl.multiple_of(me * cap, 8), lambda c: blocks[me, c], power_row)

    def finish(at, j):
        ask_copy(at, j, j).wait_send()
        pow_copy(at, j, j).wait()
        sum_copy(at, j, j).wait()

    others(finish, -1)


def thermal_kernel(
    scale, wanted, potential_in, arrived, sums, temp_old, heat_cap, conduct,
    temp_new, potential, heat, sem,
):
    through = pltpu.make_async_copy(potential_in, potential, sem)
    through.start()
    n, cap = wanted.shape
    count = temp_old.shape[0]
    factor = scale / jnp.sum(sums[...])

    def land(j, carry):
        for c in range(cap):
            heat[pl.ds(wanted[j, c] + 7, 1), :] = arrived[pl.ds(j * cap + c, 1), :]
        return carry

    lax.fori_loop(0, n, land, 0, unroll=2)
    step = 256

    def solve(b, carry):
        at = pl.ds(pl.multiple_of(b * step, 8), step)
        k = conduct[at, :]
        left = 0.5 * (k + shifted(k, 1, 1, False))
        right = 0.5 * (k + shifted(k, -1, 1, False))
        lane = lax.broadcasted_iota(jnp.int32, k.shape, 1)
        left = jnp.where(lane == 0, 0.0, left)
        right = jnp.where(lane == k.shape[1] - 1, 0.0, right)
        cap_here = heat_cap[at, :]
        total = cap_here + left + right
        old = temp_old[at, :]
        target = cap_here * old + heat[pl.ds(pl.multiple_of(b * step + 8, 8), step), :] * factor
        current = old
        for _ in range(JACOBI):
            before = shifted(current, 1, 1, True)
            after = shifted(current, -1, 1, True)
            current = (target + left * before + right * after) / total
        temp_new[at, :] = current
        return carry

    lax.fori_loop(0, count // step, solve, 0)
    through.wait()


def per_device(source, sigma_ref, owner, slot, temp_old, heat_cap, conduct):
    layers, blks = lax.axis_size("layer"), lax.axis_size("blk")
    peers = layers * blks
    ca, cr, lanes = source.shape
    count = temp_old.shape[0]
    positions, slot_code, block_code = routing(owner, slot, peers)
    cap = slot_code.shape[1]
    ask = jnp.pad(slot_code, ((0, 0), (0, 128 - cap)))[:, None, :]
    ext = pltpu.VMEM((ca + 2 * WIDE, cr + 2 * ROWS, lanes), jnp.float32)
    vmem, smem = pl.BlockSpec(memory_space=pltpu.VMEM), pl.BlockSpec(memory_space=pltpu.SMEM)
    each = pltpu.SemaphoreType.DMA((peers,))

    def kernel(*refs):
        exchange_kernel(layers, blks, ca, *refs)

    potential, arrived, wanted, sums = pl.pallas_call(
        kernel,
        out_shape=(
            jax.ShapeDtypeStruct(source.shape, jnp.float32),
            jax.ShapeDtypeStruct((peers * cap, lanes), jnp.float32),
            jax.ShapeDtypeStruct((peers, 1, 128), jnp.int32),
            jax.ShapeDtypeStruct((peers, 1, lanes), jnp.float32),
        ),
        in_specs=[vmem] * 4 + [smem] * 2,
        out_specs=(vmem,) * 4,
        scratch_shapes=[
            pltpu.SMEM((peers, 1, 128), jnp.int32),
            pltpu.VMEM((peers * cap, lanes), jnp.float32),
            pltpu.VMEM((peers * cap, lanes), jnp.float32),
            ext, ext, ext, ext, ext, ext, ext,
            pltpu.VMEM((ca * cr, lanes), jnp.float32),
            pltpu.VMEM((1, lanes), jnp.float32),
            pltpu.SemaphoreType.DMA((3,)),
            each, each, each, each, each, each, each, each,
            pltpu.SemaphoreType.DMA((2, 8)),
            pltpu.SemaphoreType.DMA((2, 8)),
        ],
        compiler_params=pltpu.CompilerParams(
            collective_id=0, has_side_effects=True, vmem_limit_bytes=40 << 20
        ),
    )(source, sigma_ref, temp_old, ask, positions.reshape(ca, cr), block_code)
    scale = source.size * peers

    def heat_step(*refs):
        thermal_kernel(float(scale), *refs)

    whole = pl.BlockSpec(memory_space=pl.ANY)
    temp_new, potential = pl.pallas_call(
        heat_step,
        out_shape=(
            jax.ShapeDtypeStruct(temp_old.shape, jnp.float32),
            jax.ShapeDtypeStruct(source.shape, jnp.float32),
        ),
        in_specs=[smem, whole] + [vmem] * 5,
        out_specs=(vmem, whole),
        scratch_shapes=[
            pltpu.VMEM((count + 8, lanes), jnp.float32),
            pltpu.SemaphoreType.DMA(()),
        ],
        compiler_params=pltpu.CompilerParams(vmem_limit_bytes=40 << 20),
    )(wanted[:, 0, :cap], potential, arrived, sums, temp_old, heat_cap, conduct)
    return (potential, temp_new)


def solution(mesh):
    return jax.shard_map(
        per_device,
        mesh=mesh,
        in_specs=(
            P("layer", "blk", None),
            P("layer", "blk", None),
            P("layer", "blk"),
            P("layer", "blk"),
            P(("blk", "layer"), None),
            P(("blk", "layer"), None),
            P(("blk", "layer"), None),
        ),
        out_specs=(P("layer", "blk", None), P(("blk", "layer"), None)),
        check_vma=False,
    )
```
